32 devices in a mesh: groups: 2 (over y), fsdp: 2 (over core), ep: 8 (over z, x).
Axes of the slice: x: 2, y: 2, z: 4, core: 2. Of those that a mesh axis runs over, the one named last changes fastest.
Arguments:
- tokens: bfloat16 [32, 7168], P(('groups', 'fsdp', 'ep')), parts along dimension 0, may hold values from -6 to 6
- gate_weight: bfloat16 [7168, 1024], P('fsdp', 'ep'), may hold values from -0.0625 to 0.0625
- up_weight: bfloat16 [7168, 1024], P('fsdp', 'ep'), may hold values from -0.0625 to 0.0625
- down_weight: bfloat16 [1024, 7168], P('ep', 'fsdp'), may hold values from -0.1875 to 0.1875
- steering: bfloat16 [1, 7168], replicated, may hold values from -3 to 3
- block_rows: int32 [2, 2, 8], P(None, 'groups'), parts along dimension 1, may hold values from 0 to 7, as said below
- block_gates: float32 [2, 2, 8], P(None, 'groups'), parts along dimension 1, may hold values from 0 to 1, as said below
Outputs:
- mixed: bfloat16 [32, 7168], P(('groups', 'fsdp', 'ep')), parts along dimension 0
The draws below stay inside these ranges and needn't reach their ends.
There are 2 independent parts, one for each index of `groups`. The reference program is written for one: setup_inputs(seed, part) draws one part's arguments, and reference() takes and returns one part's arrays. A program takes and returns all parts, laid end to end along the dimension named above; an argument that names none is the same for every part. Nothing has to cross between parts.
Inputs may be any that keep to these rules, and one draw needn't show every extreme that they name: `block_rows`: within one block the 8 token numbers are distinct. `block_gates`: in each block the gates are positive and falling on the first slots and zero on the rest; in each half one block has no zero gate.
All inputs are finite; a program needn't handle non-finite values.
Results may differ from the reference program's by a relative error of at most 0.0049.
Values may be sent and summed in bfloat16 or wider, within the bound.
No kernel may reach another device: no remote copies, remote signals or barrier semaphores. Data moves between devices by JAX's collectives and lax.ppermute only.
A program may use at most 64 MiB of HBM per device.

```python
import jax
import jax.numpy as jnp

D = 7168
FW = 1024
E_WIN = 1
TOKENS_H = 8
TOKENS = 16
BLK = 8
N_FSDP = 2


def routing_parts(key):
    seeded = jax.random.fold_in(key, 17)
    perm_key, load_key, hot_key, gate_key = jax.random.split(seeded, 4)
    subkeys = jax.random.split(perm_key, N_FSDP * E_WIN)
    shuffled = jax.vmap(lambda subkey: jax.random.permutation(subkey, TOKENS_H)[:BLK])(subkeys)
    row_table = shuffled.reshape(N_FSDP, E_WIN, BLK).astype(jnp.int32)
    live_loads = jax.random.randint(load_key, (N_FSDP, E_WIN), max(1, BLK // 8), BLK // 2 + 1)
    hot_expert = jax.random.randint(hot_key, (N_FSDP,), 0, E_WIN)
    live_loads = jnp.where(jnp.arange(E_WIN)[None, :] == hot_expert[:, None], BLK, live_loads)
    return (row_table, live_loads, gate_key)


def draw_block_rows(key, part):
    row_table, live_loads, gate_key = routing_parts(key)
    return row_table


def draw_block_gates(key, part):
    row_table, live_loads, gate_key = routing_parts(key)
    raw_gates = jax.random.uniform(gate_key, (N_FSDP, E_WIN, BLK), jnp.float32, 0.2, 1.0)
    raw_gates = -jnp.sort(-raw_gates, axis=2)
    live_slots = jnp.arange(BLK)[None, None, :] < live_loads[:, :, None]
    return jnp.where(live_slots, raw_gates, 0.0).astype(jnp.float32)


def steps_of(stream_key, extent, shards, low, largest):
    gain = 1.0
    for axis_at, parts in shards:
        steps = jax.random.uniform(jax.random.fold_in(jax.random.fold_in(stream_key, 6), axis_at), (parts,), jnp.float32, low / len(shards), largest / len(shards))
        gain = gain * jnp.repeat(jnp.exp(steps), extent[axis_at] // parts).reshape((-1,) + (1,) * (len(extent) - 1 - axis_at))
    return gain


def bell_draw(key, shape, scale, reach, shards=(), held_as=jnp.bfloat16):
    level = steps_of(key, shape, shards, -0.22, 0.18) if shards else 1.0
    drawn = jax.random.normal(key, shape, jnp.float32) * scale * level
    return jnp.minimum(jnp.maximum(drawn, -reach), reach).astype(held_as)


def setup_inputs(seed: int = 0, part: int = 0) -> dict:
    seeds = jax.random.split(jax.random.key(seed), 8)
    own_keys = jax.random.split(jax.random.fold_in(seeds[7], part), 8)
    tokens = bell_draw(own_keys[0], (TOKENS, D), 1.0, 6.0, ((0, 16),))
    gate_weight = bell_draw(seeds[1], (D, E_WIN * FW), D ** -0.5, 0.0625, ((0, 2), (1, 8)))
    up_weight = bell_draw(seeds[2], (D, E_WIN * FW), D ** -0.5, 0.0625, ((0, 2), (1, 8)))
    down_weight = bell_draw(seeds[3], (E_WIN * FW, D), FW ** -0.5, 0.1875, ((0, 8), (1, 2)))
    steering = bell_draw(seeds[4], (E_WIN, D), 0.5, 3.0)
    block_rows = draw_block_rows(jax.random.fold_in(jax.random.fold_in(seeds[7], part), 71), part)
    block_gates = draw_block_gates(jax.random.fold_in(jax.random.fold_in(seeds[7], part), 71), part)
    return dict(tokens=tokens, gate_weight=gate_weight, up_weight=up_weight, down_weight=down_weight, steering=steering, block_rows=block_rows, block_gates=block_gates)


def reference(tokens, gate_weight, up_weight, down_weight, steering, block_rows, block_gates):
    outputs = []
    for half in range(N_FSDP):
        half_tokens = tokens[half * TOKENS_H:(half + 1) * TOKENS_H]
        accum = jnp.zeros((TOKENS_H, D), jnp.float32)
        for expert in range(E_WIN):
            slot_rows = block_rows[half, expert]
            slot_gates = block_gates[half, expert]
            picked = jnp.take(half_tokens, slot_rows, axis=0)
            gate_pre = jnp.dot(picked, gate_weight[:, expert * FW:(expert + 1) * FW], preferred_element_type=jnp.float32)
            up_pre = jnp.dot(picked, up_weight[:, expert * FW:(expert + 1) * FW], preferred_element_type=jnp.float32)
            hidden = (jax.nn.silu(gate_pre) * up_pre).astype(jnp.bfloat16)
            projected = jnp.dot(hidden, down_weight[expert * FW:(expert + 1) * FW], preferred_element_type=jnp.float32)
            weighted = slot_gates[:, None] * (projected + steering[expert].astype(jnp.float32)[None, :])
            accum = accum.at[slot_rows].add(weighted)
        outputs.append(accum)
    return jnp.concatenate(outputs, axis=0).astype(jnp.bfloat16)
```

```python
import jax
import jax.numpy as jnp
from jax import lax
from jax.sharding import PartitionSpec as P


def partner(x, axis, distance):
    count = lax.axis_size(axis)
    return lax.ppermute(x, axis, [(i, i ^ distance) for i in range(count)])


def distances(count):
    found = []
    step = count // 2
    while step:
        found.append(step)
        step //= 2
    return found


def gather_rows(row, axis):
    rows = row
    owners = [0]
    for d in distances(lax.axis_size(axis)):
        rows = jnp.concatenate([rows, partner(rows, axis, d)], axis=0)
        owners = owners + [o ^ d for o in owners]
    return rows, owners


def scatter_sum(rows, axis):
    for d in reversed(distances(lax.axis_size(axis))):
        kept = rows.shape[0] // 2
        got = partner(rows[kept:].astype(jnp.bfloat16), axis, d)
        rows = rows[:kept] + got.astype(jnp.float32)
    return rows


def dot(a, b):
    return jnp.dot(a, b, preferred_element_type=jnp.float32)


def body(tokens, gate_weight, up_weight, down_weight, steering, block_rows, block_gates):
    window_experts = block_rows.shape[1]
    group_size = lax.axis_size("ep") // window_experts
    position = lax.axis_index("ep")
    expert = position // group_size
    half = lax.axis_index("fsdp")
    half_slots = lax.dynamic_index_in_dim(block_rows, half, 0, keepdims=False)
    half_gates = lax.dynamic_index_in_dim(block_gates, half, 0, keepdims=False)

    own_gate = jnp.sum(jnp.where(half_slots == position, half_gates, 0.0), axis=1)
    steer = jnp.sum(own_gate[:, None] * steering.astype(jnp.float32), axis=0, keepdims=True)

    gate_far = partner(gate_weight, "fsdp", 1)
    up_far = partner(up_weight, "fsdp", 1)
    down_far = partner(down_weight, "fsdp", 1)
    rows, owners = gather_rows(tokens, "ep")

    slots = lax.dynamic_index_in_dim(half_slots, expert, 0, keepdims=False)
    gates = lax.dynamic_index_in_dim(half_gates, expert, 0, keepdims=False)
    token = position ^ jnp.asarray(owners)
    token_gate = jnp.sum(jnp.where(slots[None, :] == token[:, None], gates[None, :], 0.0), axis=1, keepdims=True)

    width = tokens.shape[1] // 2
    near = lax.dynamic_slice_in_dim(rows, half * width, width, 1)
    far = lax.dynamic_slice_in_dim(rows, (1 - half) * width, width, 1)
    gate_pre = dot(near, gate_weight) + dot(far, gate_far)
    up_pre = dot(near, up_weight) + dot(far, up_far)
    hidden = (jax.nn.silu(gate_pre) * up_pre).astype(jnp.bfloat16)
    down_near = dot(hidden, down_weight)
    down_other = dot(hidden, down_far)
    first = half == 0
    projected = jnp.concatenate(
        [jnp.where(first, down_near, down_other), jnp.where(first, down_other, down_near)], axis=1
    )
    summed = scatter_sum(token_gate * projected, "ep")
    return (summed + steer).astype(jnp.bfloat16)


def solution(mesh):
    placed = (
        P(("groups", "fsdp", "ep"), None),
        P("fsdp", "ep"),
        P("fsdp", "ep"),
        P("ep", "fsdp"),
        P(),
        P(None, "groups", None),
        P(None, "groups", None),
    )
    return jax.shard_map(
        body,
        mesh=mesh,
        in_specs=placed,
        out_specs=P(("groups", "fsdp", "ep"), None),
        check_vma=False,
    )
```

```python
import functools

import jax
import jax.numpy as jnp
from jax import lax
from jax.experimental import pallas as pl
from jax.experimental.pallas import tpu as pltpu
from jax.sharding import PartitionSpec as P

VMEM_LIMIT = 48 * 2**20


def swap_cores(x):
    return lax.ppermute(x, "fsdp", [(0, 1), (1, 0)])


def exchange(x, distance, cross):
    count = lax.axis_size("ep")
    pairs = [(f * count + e, (f ^ cross) * count + (e ^ distance)) for f in range(2) for e in range(count)]
    return lax.ppermute(x, ("fsdp", "ep"), pairs)


def stages(count):
    steps = [(1, 2, 1)] if count > 1 else []
    base = 2
    while base < count:
        radix = 4 if base * 4 <= count else 2
        steps.append((base, radix, 1))
        base *= radix
    return steps


def dot(a, b):
    return jnp.dot(a, b, preferred_element_type=jnp.float32)


def stage_kernel(*refs):
    count = len(refs) // 2
    copies = [pltpu.make_async_copy(refs[i], refs[count + i], refs[-1].at[i]) for i in range(count)]
    for copy in copies:
        copy.start()
    for copy in copies:
        copy.wait()


def stage(*arrays):
    return pl.pallas_call(
        stage_kernel,
        out_shape=[jax.ShapeDtypeStruct(a.shape, a.dtype) for a in arrays],
        in_specs=[pl.BlockSpec(memory_space=pltpu.HBM)] * len(arrays),
        out_specs=[pl.BlockSpec(memory_space=pltpu.VMEM)] * len(arrays),
        scratch_shapes=[pltpu.SemaphoreType.DMA((len(arrays),))],
        compiler_params=pltpu.CompilerParams(vmem_limit_bytes=VMEM_LIMIT),
        name="stage",
    )(*[pltpu.with_memory_space_constraint(a, pltpu.HBM) for a in arrays])


def experts_kernel(owners, pieces, *refs):
    row_refs = refs[:pieces]
    gate_ref, up_ref, down_ref, steer_ref, slots_ref, gates_ref, gate_far_ref, up_far_ref, down_far_ref = refs[pieces:pieces + 9]
    keep_ref = refs[pieces + 9]
    send_refs = refs[pieces + 10:2 * pieces + 9]
    rows_scr, out_scr = refs[2 * pieces + 9:]
    window_experts = slots_ref.shape[1]
    position = lax.axis_index("ep")
    half = lax.axis_index("fsdp")
    expert = position // (lax.axis_size("ep") // window_experts)
    count = len(owners)
    chunk = count // pieces
    width = gate_ref.shape[0]
    near = pl.multiple_of(half * width, 128)
    far = pl.multiple_of((1 - half) * width, 128)
    for k, ref in enumerate(row_refs):
        rows_scr[k * chunk:(k + 1) * chunk, :] = ref[...].astype(jnp.float32)
    x_near = rows_scr[:, pl.ds(near, width)].astype(jnp.bfloat16)
    x_far = rows_scr[:, pl.ds(far, width)].astype(jnp.bfloat16)
    gate_pre = dot(x_near, gate_ref[...]) + dot(x_far, gate_far_ref[...])
    up_pre = dot(x_near, up_ref[...]) + dot(x_far, up_far_ref[...])
    hidden = (gate_pre / (1.0 + jnp.exp(-gate_pre)) * up_pre).astype(jnp.bfloat16)
    row = lax.broadcasted_iota(jnp.int32, (count, 1), 0)
    offset = jnp.zeros((count, 1), jnp.int32)
    other = jnp.zeros((count, 1), jnp.int32)
    for j, (o, c) in enumerate(owners):
        if o:
            offset = jnp.where(row == j, o, offset)
        if c:
            other = jnp.where(row == j, 1, other)
    token = position ^ offset
    row_half = half ^ other
    token_gate = jnp.zeros((count, 1), jnp.float32)
    for h in range(2):
        slots = slots_ref[h, pl.ds(expert, 1), :]
        gates = gates_ref[h, pl.ds(expert, 1), :]
        found = jnp.sum(jnp.where(slots == token, gates, 0.0), axis=1, keepdims=True)
        token_gate = jnp.where(row_half == h, found, token_gate)
    out_scr[:, pl.ds(near, width)] = token_gate * dot(hidden, down_ref[...])
    out_scr[:, pl.ds(far, width)] = token_gate * dot(hidden, down_far_ref[...])
    own_gate = jnp.sum(jnp.where(slots_ref[half] == position, gates_ref[half], 0.0), axis=1, keepdims=True)
    steer = jnp.sum(own_gate * steer_ref[...].astype(jnp.float32), axis=0, keepdims=True)
    out_scr[0:1, :] = out_scr[0:1, :] + steer
    keep_ref[...] = out_scr[0:chunk, :]
    for k, ref in enumerate(send_refs):
        ref[...] = out_scr[(k + 1) * chunk:(k + 2) * chunk, :].astype(jnp.bfloat16)


def body(tokens, gate_weight, up_weight, down_weight, steering, block_rows, block_gates):
    count = lax.axis_size("ep")
    width_all = tokens.shape[1]
    here = None
    pieces = [tokens]
    owners = [(0, 0)]
    steps = stages(count)
    for i, (base, radix, cross) in enumerate(steps):
        rows = jnp.concatenate(pieces, axis=0) if len(pieces) > 1 else pieces[0]
        if i == 1:
            here = stage(gate_weight, up_weight, down_weight, steering, block_rows, block_gates)
            rows, here = lax.optimization_barrier((rows, here))
        pieces = [rows] + [exchange(rows, k * base, cross) for k in range(1, radix)]
        owners = [(o ^ (k * base), c ^ (cross if k else 0)) for k in range(radix) for o, c in owners]
    if here is None:
        here = stage(gate_weight, up_weight, down_weight, steering, block_rows, block_gates)
    far = [swap_cores(w) for w in (gate_weight, up_weight, down_weight)]
    chunk = count // len(pieces)
    vmem = pl.BlockSpec(memory_space=pltpu.VMEM)
    outs = pl.pallas_call(
        functools.partial(experts_kernel, owners, len(pieces)),
        out_shape=[jax.ShapeDtypeStruct((chunk, width_all), jnp.float32)]
        + [jax.ShapeDtypeStruct((chunk, width_all), jnp.bfloat16)] * (len(pieces) - 1),
        in_specs=[vmem] * (len(pieces) + 9),
        out_specs=[vmem] * len(pieces),
        scratch_shapes=[pltpu.VMEM((count, width_all), jnp.float32), pltpu.VMEM((count, width_all), jnp.float32)],
        compiler_params=pltpu.CompilerParams(vmem_limit_bytes=VMEM_LIMIT),
        name="experts",
    )(*pieces, *here, *far)
    total, sends = outs[0], list(outs[1:])
    for i, (base, radix, cross) in enumerate(reversed(steps)):
        if i:
            chunk = total.shape[0] // radix
            sends = [total[k * chunk:(k + 1) * chunk].astype(jnp.bfloat16) for k in range(1, radix)]
            total = total[:chunk]
        got = [exchange(s, k * base, cross) for k, s in enumerate(sends, 1)]
        for g in got:
            total = total + g.astype(jnp.float32)
    return total.astype(jnp.bfloat16)


def solution(mesh):
    placed = (
        P(("groups", "fsdp", "ep"), None),
        P("fsdp", "ep"),
        P("fsdp", "ep"),
        P("ep", "fsdp"),
        P(),
        P(None, "groups", None),
        P(None, "groups", None),
    )
    return jax.shard_map(
        body,
        mesh=mesh,
        in_specs=placed,
        out_specs=P(("groups", "fsdp", "ep"), None),
        check_vma=False,
    )
```

```python
import functools

import jax
import jax.numpy as jnp
from jax import lax
from jax.experimental import pallas as pl
from jax.experimental.pallas import tpu as pltpu
from jax.sharding import PartitionSpec as P

VMEM_LIMIT = 48 * 2**20


def swap_cores(x):
    return lax.ppermute(x, "fsdp", [(0, 1), (1, 0)])


def exchange(x, distance, cross):
    count = lax.axis_size("ep")
    pairs = [(f * count + e, (f ^ cross) * count + (e ^ distance)) for f in range(2) for e in range(count)]
    return lax.ppermute(x, ("fsdp", "ep"), pairs)


def stages(count):
    steps = [(1, 2, 1)] if count > 1 else []
    base = 2
    while base < count:
        radix = 4 if base * 4 <= count else 2
        steps.append((base, radix, 1))
        base *= radix
    return steps


def dot(a, b):
    return jnp.dot(a, b, preferred_element_type=jnp.float32)


def stage_kernel(*refs):
    count = len(refs) // 2
    copies = [pltpu.make_async_copy(refs[i], refs[count + i], refs[-1].at[i]) for i in range(count)]
    for copy in copies:
        copy.start()
    for copy in copies:
        copy.wait()


def stage(*arrays):
    return pl.pallas_call(
        stage_kernel,
        out_shape=[jax.ShapeDtypeStruct(a.shape, a.dtype) for a in arrays],
        in_specs=[pl.BlockSpec(memory_space=pltpu.HBM)] * len(arrays),
        out_specs=[pl.BlockSpec(memory_space=pltpu.VMEM)] * len(arrays),
        scratch_shapes=[pltpu.SemaphoreType.DMA((len(arrays),))],
        compiler_params=pltpu.CompilerParams(vmem_limit_bytes=VMEM_LIMIT),
        name="stage",
    )(*[pltpu.with_memory_space_constraint(a, pltpu.HBM) for a in arrays])


def experts_kernel(owners, pieces, *refs):
    row_refs = refs[:pieces]
    gate_ref, up_ref, down_ref, steer_ref, slots_ref, gates_ref, gate_far_ref, up_far_ref, down_far_ref = refs[pieces:pieces + 9]
    keep_ref = refs[pieces + 9]
    send_refs = refs[pieces + 10:2 * pieces + 9]
    rows_scr, out_scr = refs[2 * pieces + 9:]
    window_experts = slots_ref.shape[1]
    position = lax.axis_index("ep")
    half = lax.axis_index("fsdp")
    expert = position // (lax.axis_size("ep") // window_experts)
    count = len(owners)
    chunk = count // pieces
    width = gate_ref.shape[0]
    near = pl.multiple_of(half * width, 128)
    far = pl.multiple_of((1 - half) * width, 128)
    for k, ref in enumerate(row_refs):
        rows_scr[k * chunk:(k + 1) * chunk, :] = ref[...].astype(jnp.float32)
    x_near = rows_scr[:, pl.ds(near, width)].astype(jnp.bfloat16)
    x_far = rows_scr[:, pl.ds(far, width)].astype(jnp.bfloat16)
    gate_pre = dot(x_near, gate_ref[...]) + dot(x_far, gate_far_ref[...])
    up_pre = dot(x_near, up_ref[...]) + dot(x_far, up_far_ref[...])
    hidden = (gate_pre / (1.0 + jnp.exp(-gate_pre)) * up_pre).astype(jnp.bfloat16)
    row = lax.broadcasted_iota(jnp.int32, (count, 1), 0)
    offset = jnp.zeros((count, 1), jnp.int32)
    other = jnp.zeros((count, 1), jnp.int32)
    for j, (o, c) in enumerate(owners):
        if o:
            offset = jnp.where(row == j, o, offset)
        if c:
            other = jnp.where(row == j, 1, other)
    token = position ^ offset
    row_half = half ^ other
    token_gate = jnp.zeros((count, 1), jnp.float32)
    for h in range(2):
        slots = slots_ref[h, pl.ds(expert, 1), :]
        gates = gates_ref[h, pl.ds(expert, 1), :]
        found = jnp.sum(jnp.where(slots == token, gates, 0.0), axis=1, keepdims=True)
        token_gate = jnp.where(row_half == h, found, token_gate)
    out_scr[:, pl.ds(near, width)] = token_gate * dot(hidden, down_ref[...])
    out_scr[:, pl.ds(far, width)] = token_gate * dot(hidden, down_far_ref[...])
    own_gate = jnp.sum(jnp.where(slots_ref[half] == position, gates_ref[half], 0.0), axis=1, keepdims=True)
    steer = jnp.sum(own_gate * steer_ref[...].astype(jnp.float32), axis=0, keepdims=True)
    out_scr[0:1, :] = out_scr[0:1, :] + steer
    keep_ref[...] = out_scr[0:chunk, :]
    for k, ref in enumerate(send_refs):
        ref[...] = out_scr[(k + 1) * chunk:(k + 2) * chunk, :].astype(jnp.bfloat16)


def body(tokens, gate_weight, up_weight, down_weight, steering, block_rows, block_gates):
    count = lax.axis_size("ep")
    width_all = tokens.shape[1]
    here = None
    pieces = [tokens]
    owners = [(0, 0)]
    steps = stages(count)
    for i, (base, radix, cross) in enumerate(steps):
        rows = jnp.concatenate(pieces, axis=0) if len(pieces) > 1 else pieces[0]
        if i == 1:
            here = stage(gate_weight, up_weight, down_weight, steering, block_rows, block_gates)
            far = {n: swap_cores(w) for n, w in zip("gud", (gate_weight, up_weight, down_weight))}
            rows, here, early = lax.optimization_barrier((rows, here, [far[n] for n in "g"]))
            far.update(zip("g", early))
        pieces = [rows] + [exchange(rows, k * base, cross) for k in range(1, radix)]
        owners = [(o ^ (k * base), c ^ (cross if k else 0)) for k in range(radix) for o, c in owners]
    if here is None:
        here = stage(gate_weight, up_weight, down_weight, steering, block_rows, block_gates)
    far = [far[n] for n in "gud"]
    chunk = count // len(pieces)
    vmem = pl.BlockSpec(memory_space=pltpu.VMEM)
    outs = pl.pallas_call(
        functools.partial(experts_kernel, owners, len(pieces)),
        out_shape=[jax.ShapeDtypeStruct((chunk, width_all), jnp.float32)]
        + [jax.ShapeDtypeStruct((chunk, width_all), jnp.bfloat16)] * (len(pieces) - 1),
        in_specs=[vmem] * (len(pieces) + 9),
        out_specs=[vmem] * len(pieces),
        scratch_shapes=[pltpu.VMEM((count, width_all), jnp.float32), pltpu.VMEM((count, width_all), jnp.float32)],
        compiler_params=pltpu.CompilerParams(vmem_limit_bytes=VMEM_LIMIT),
        name="experts",
    )(*pieces, *here, *far)
    total, sends = outs[0], list(outs[1:])
    for i, (base, radix, cross) in enumerate(reversed(steps)):
        if i:
            chunk = total.shape[0] // radix
            sends = [total[k * chunk:(k + 1) * chunk].astype(jnp.bfloat16) for k in range(1, radix)]
            total = total[:chunk]
        got = [exchange(s, k * base, cross) for k, s in reversed(list(enumerate(sends, 1)))]
        for g in got:
            total = total + g.astype(jnp.float32)
    return total.astype(jnp.bfloat16)


def solution(mesh):
    placed = (
        P(("groups", "fsdp", "ep"), None),
        P("fsdp", "ep"),
        P("fsdp", "ep"),
        P("ep", "fsdp"),
        P(),
        P(None, "groups", None),
        P(None, "groups", None),
    )
    return jax.shard_map(
        body,
        mesh=mesh,
        in_specs=placed,
        out_specs=P(("groups", "fsdp", "ep"), None),
        check_vma=False,
    )
```

```python
import functools

import jax
import jax.numpy as jnp
from jax import lax
from jax.experimental import pallas as pl
from jax.experimental.pallas import tpu as pltpu
from jax.sharding import PartitionSpec as P

VMEM_LIMIT = 48 * 2**20


def swap_cores(x):
    return lax.ppermute(x, "fsdp", [(0, 1), (1, 0)])


def exchange(x, distance, cross):
    count = lax.axis_size("ep")
    pairs = [(f * count + e, (f ^ cross) * count + (e ^ distance)) for f in range(2) for e in range(count)]
    return lax.ppermute(x, ("fsdp", "ep"), pairs)


def stages(count):
    if count == 8:
        return [[(4, 1)], [(1, 1), (2, 1), (3, 1)]]
    plan = [[(1, 1)]] if count > 1 else []
    base = 2
    while base < count:
        radix = 4 if base * 4 <= count else 2
        plan.append([(k * base, 1) for k in range(1, radix)])
        base *= radix
    return plan


def dot(a, b):
    return jnp.dot(a, b, preferred_element_type=jnp.float32)


def stage_kernel(*refs):
    count = len(refs) // 2
    copies = [pltpu.make_async_copy(refs[i], refs[count + i], refs[-1].at[i]) for i in range(count)]
    for copy in copies:
        copy.start()
    for copy in copies:
        copy.wait()


def stage(*arrays):
    return pl.pallas_call(
        stage_kernel,
        out_shape=[jax.ShapeDtypeStruct(a.shape, a.dtype) for a in arrays],
        in_specs=[pl.BlockSpec(memory_space=pltpu.HBM)] * len(arrays),
        out_specs=[pl.BlockSpec(memory_space=pltpu.VMEM)] * len(arrays),
        scratch_shapes=[pltpu.SemaphoreType.DMA((len(arrays),))],
        compiler_params=pltpu.CompilerParams(vmem_limit_bytes=VMEM_LIMIT),
        name="stage",
    )(*[pltpu.with_memory_space_constraint(a, pltpu.HBM) for a in arrays])


def experts_kernel(owners, pieces, *refs):
    row_refs = refs[:pieces]
    gate_ref, up_ref, down_ref, steer_ref, slots_ref, gates_ref, gate_far_ref, up_far_ref, down_far_ref = refs[pieces:pieces + 9]
    keep_ref = refs[pieces + 9]
    send_refs = refs[pieces + 10:2 * pieces + 9]
    rows_scr, out_scr = refs[2 * pieces + 9:]
    window_experts = slots_ref.shape[1]
    position = lax.axis_index("ep")
    half = lax.axis_index("fsdp")
    expert = position // (lax.axis_size("ep") // window_experts)
    count = len(owners)
    chunk = count // pieces
    width = gate_ref.shape[0]
    near = pl.multiple_of(half * width, 128)
    far = pl.multiple_of((1 - half) * width, 128)
    for k, ref in enumerate(row_refs):
        rows_scr[k * chunk:(k + 1) * chunk, :] = ref[...].astype(jnp.float32)
    x_near = rows_scr[:, pl.ds(near, width)].astype(jnp.bfloat16)
    x_far = rows_scr[:, pl.ds(far, width)].astype(jnp.bfloat16)
    gate_pre = dot(x_near, gate_ref[...]) + dot(x_far, gate_far_ref[...])
    up_pre = dot(x_near, up_ref[...]) + dot(x_far, up_far_ref[...])
    hidden = (gate_pre / (1.0 + jnp.exp(-gate_pre)) * up_pre).astype(jnp.bfloat16)
    row = lax.broadcasted_iota(jnp.int32, (count, 1), 0)
    offset = jnp.zeros((count, 1), jnp.int32)
    other = jnp.zeros((count, 1), jnp.int32)
    for j, (o, c) in enumerate(owners):
        if o:
            offset = jnp.where(row == j, o, offset)
        if c:
            other = jnp.where(row == j, 1, other)
    token = position ^ offset
    row_half = half ^ other
    token_gate = jnp.zeros((count, 1), jnp.float32)
    for h in range(2):
        slots = slots_ref[h, pl.ds(expert, 1), :]
        gates = gates_ref[h, pl.ds(expert, 1), :]
        found = jnp.sum(jnp.where(slots == token, gates, 0.0), axis=1, keepdims=True)
        token_gate = jnp.where(row_half == h, found, token_gate)
    out_scr[:, pl.ds(near, width)] = token_gate * dot(hidden, down_ref[...])
    out_scr[:, pl.ds(far, width)] = token_gate * dot(hidden, down_far_ref[...])
    own_gate = jnp.sum(jnp.where(slots_ref[half] == position, gates_ref[half], 0.0), axis=1, keepdims=True)
    steer = jnp.sum(own_gate * steer_ref[...].astype(jnp.float32), axis=0, keepdims=True)
    out_scr[0:1, :] = out_scr[0:1, :] + steer
    keep_ref[...] = out_scr[0:chunk, :]
    for k, ref in enumerate(send_refs):
        ref[...] = out_scr[(k + 1) * chunk:(k + 2) * chunk, :].astype(jnp.bfloat16)


def body(tokens, gate_weight, up_weight, down_weight, steering, block_rows, block_gates):
    count = lax.axis_size("ep")
    width_all = tokens.shape[1]
    here = None
    pieces = [tokens]
    owners = [(0, 0)]
    steps = stages(count)
    for i, hops in enumerate(steps):
        rows = jnp.concatenate(pieces, axis=0) if len(pieces) > 1 else pieces[0]
        if i == 1:
            here = stage(gate_weight, up_weight, down_weight, steering, block_rows, block_gates)
            far = {n: swap_cores(w) for n, w in zip("gud", (gate_weight, up_weight, down_weight))}
            rows, here, early = lax.optimization_barrier((rows, here, [far[n] for n in "g"]))
            far.update(zip("g", early))
        pieces = [rows] + [exchange(rows, d, c) for d, c in hops]
        owners = owners + [(o ^ d, c ^ x) for d, x in hops for o, c in owners]
    if here is None:
        here = stage(gate_weight, up_weight, down_weight, steering, block_rows, block_gates)
    far = [far[n] for n in "gud"]
    chunk = count // len(pieces)
    vmem = pl.BlockSpec(memory_space=pltpu.VMEM)
    outs = pl.pallas_call(
        functools.partial(experts_kernel, owners, len(pieces)),
        out_shape=[jax.ShapeDtypeStruct((chunk, width_all), jnp.float32)]
        + [jax.ShapeDtypeStruct((chunk, width_all), jnp.bfloat16)] * (len(pieces) - 1),
        in_specs=[vmem] * (len(pieces) + 9),
        out_specs=[vmem] * len(pieces),
        scratch_shapes=[pltpu.VMEM((count, width_all), jnp.float32), pltpu.VMEM((count, width_all), jnp.float32)],
        compiler_params=pltpu.CompilerParams(vmem_limit_bytes=VMEM_LIMIT),
        name="experts",
    )(*pieces, *here, *far)
    total, sends = outs[0], list(outs[1:])
    for i, hops in enumerate(reversed(steps)):
        if i:
            chunk = total.shape[0] // (len(hops) + 1)
            sends = [total[(k + 1) * chunk:(k + 2) * chunk].astype(jnp.bfloat16) for k in range(len(hops))]
            total = total[:chunk]
        got = [exchange(s, d, c) for s, (d, c) in reversed(list(zip(sends, hops)))]
        for g in got:
            total = total + g.astype(jnp.float32)
    return total.astype(jnp.bfloat16)


def solution(mesh):
    placed = (
        P(("groups", "fsdp", "ep"), None),
        P("fsdp", "ep"),
        P("fsdp", "ep"),
        P("ep", "fsdp"),
        P(),
        P(None, "groups", None),
        P(None, "groups", None),
    )
    return jax.shard_map(
        body,
        mesh=mesh,
        in_specs=placed,
        out_specs=P(("groups", "fsdp", "ep"), None),
        check_vma=False,
    )
```

```python
import functools

import jax
import jax.numpy as jnp
from jax import lax
from jax.experimental import pallas as pl
from jax.experimental.pallas import tpu as pltpu
from jax.sharding import PartitionSpec as P

VMEM_LIMIT = 48 * 2**20


def swap_cores(x):
    return lax.ppermute(x, "fsdp", [(0, 1), (1, 0)])


def exchange(x, distance, cross):
    count = lax.axis_size("ep")
    pairs = [(f * count + e, (f ^ cross) * count + (e ^ distance)) for f in range(2) for e in range(count)]
    return lax.ppermute(x, ("fsdp", "ep"), pairs)


def stages(count):
    if count == 8:
        return [[(4, 1)], [(1, 1), (2, 1), (3, 1)]]
    plan = [[(1, 1)]] if count > 1 else []
    base = 2
    while base < count:
        radix = 4 if base * 4 <= count else 2
        plan.append([(k * base, 1) for k in range(1, radix)])
        base *= radix
    return plan


def dot(a, b):
    return jnp.dot(a, b, preferred_element_type=jnp.float32)


def stage_kernel(*refs):
    count = len(refs) // 2
    copies = [pltpu.make_async_copy(refs[i], refs[count + i], refs[-1].at[i]) for i in range(count)]
    for copy in copies:
        copy.start()
    for copy in copies:
        copy.wait()


def stage(*arrays):
    return pl.pallas_call(
        stage_kernel,
        out_shape=[jax.ShapeDtypeStruct(a.shape, a.dtype) for a in arrays],
        in_specs=[pl.BlockSpec(memory_space=pltpu.HBM)] * len(arrays),
        out_specs=[pl.BlockSpec(memory_space=pltpu.VMEM)] * len(arrays),
        scratch_shapes=[pltpu.SemaphoreType.DMA((len(arrays),))],
        compiler_params=pltpu.CompilerParams(vmem_limit_bytes=VMEM_LIMIT),
        name="stage",
    )(*[pltpu.with_memory_space_constraint(a, pltpu.HBM) for a in arrays])


def experts_kernel(owners, pieces, *refs):
    row_refs = refs[:pieces]
    gate_ref, up_ref, down_ref, steer_ref, slots_ref, gates_ref, gate_far_ref, up_far_ref, down_far_ref = refs[pieces:pieces + 9]
    keep_ref = refs[pieces + 9]
    send_refs = refs[pieces + 10:2 * pieces + 9]
    rows_scr, out_scr = refs[2 * pieces + 9:]
    window_experts = slots_ref.shape[1]
    position = lax.axis_index("ep")
    half = lax.axis_index("fsdp")
    expert = position // (lax.axis_size("ep") // window_experts)
    count = len(owners)
    chunk = count // pieces
    width = gate_ref.shape[0]
    near = pl.multiple_of(half * width, 128)
    far = pl.multiple_of((1 - half) * width, 128)
    rows_scr[...] = jnp.concatenate([ref[...] for ref in row_refs], axis=0)
    x_near = rows_scr[:, pl.ds(near, width)]
    x_far = rows_scr[:, pl.ds(far, width)]
    gate_pre = dot(x_near, gate_ref[...]) + dot(x_far, gate_far_ref[...])
    up_pre = dot(x_near, up_ref[...]) + dot(x_far, up_far_ref[...])
    hidden = (gate_pre / (1.0 + jnp.exp(-gate_pre)) * up_pre).astype(jnp.bfloat16)
    row = lax.broadcasted_iota(jnp.int32, (count, 1), 0)
    offset = jnp.zeros((count, 1), jnp.int32)
    other = jnp.zeros((count, 1), jnp.int32)
    for j, (o, c) in enumerate(owners):
        if o:
            offset = jnp.where(row == j, o, offset)
        if c:
            other = jnp.where(row == j, 1, other)
    token = position ^ offset
    row_half = half ^ other
    token_gate = jnp.zeros((count, 1), jnp.float32)
    for h in range(2):
        slots = slots_ref[h, pl.ds(expert, 1), :]
        gates = gates_ref[h, pl.ds(expert, 1), :]
        found = jnp.sum(jnp.where(slots == token, gates, 0.0), axis=1, keepdims=True)
        token_gate = jnp.where(row_half == h, found, token_gate)
    out_scr[:, pl.ds(near, width)] = token_gate * dot(hidden, down_ref[...])
    out_scr[:, pl.ds(far, width)] = token_gate * dot(hidden, down_far_ref[...])
    own_gate = jnp.sum(jnp.where(slots_ref[half] == position, gates_ref[half], 0.0), axis=1, keepdims=True)
    steer = jnp.sum(own_gate * steer_ref[...].astype(jnp.float32), axis=0, keepdims=True)
    out_scr[0:1, :] = out_scr[0:1, :] + steer
    keep_ref[...] = out_scr[0:chunk, :]
    for k, ref in enumerate(send_refs):
        ref[...] = out_scr[(k + 1) * chunk:(k + 2) * chunk, :].astype(jnp.bfloat16)


def body(tokens, gate_weight, up_weight, down_weight, steering, block_rows, block_gates):
    count = lax.axis_size("ep")
    width_all = tokens.shape[1]
    here = stage(gate_weight, up_weight, down_weight)
    own_row, *tables = stage(tokens, steering, block_rows, block_gates)
    rows = tokens
    owners = [(0, 0)]
    steps = stages(count)
    for i, hops in enumerate(steps):
        got = [exchange(rows, d, c) for d, c in hops]
        if not i:
            own_row, got[0], down_weight = lax.optimization_barrier((own_row, got[0], down_weight))
            far = [swap_cores(w) for w in (gate_weight, up_weight, down_weight)]
            own_row, got[0], far[0] = lax.optimization_barrier((own_row, got[0], far[0]))
            rows = own_row
        pieces = [rows] + got
        owners = owners + [(o ^ d, c ^ x) for d, x in hops for o, c in owners]
        if i + 1 < len(steps):
            rows = jnp.concatenate(pieces, axis=0)
    chunk = count // len(pieces)
    vmem = pl.BlockSpec(memory_space=pltpu.VMEM)
    outs = pl.pallas_call(
        functools.partial(experts_kernel, owners, len(pieces)),
        out_shape=[jax.ShapeDtypeStruct((chunk, width_all), jnp.float32)]
        + [jax.ShapeDtypeStruct((chunk, width_all), jnp.bfloat16)] * (len(pieces) - 1),
        in_specs=[vmem] * (len(pieces) + 9),
        out_specs=[vmem] * len(pieces),
        scratch_shapes=[pltpu.VMEM((count, width_all), jnp.bfloat16), pltpu.VMEM((count, width_all), jnp.float32)],
        compiler_params=pltpu.CompilerParams(vmem_limit_bytes=VMEM_LIMIT),
        name="experts",
    )(*pieces, *here, *tables, *far)
    total, sends = outs[0], list(outs[1:])
    for i, hops in enumerate(reversed(steps)):
        if i:
            chunk = total.shape[0] // (len(hops) + 1)
            sends = [total[(k + 1) * chunk:(k + 2) * chunk].astype(jnp.bfloat16).reshape(8, -1) for k in range(len(hops))]
            total = total[:chunk]
        got = [exchange(s, d, c) for s, (d, c) in reversed(list(zip(sends, hops)))]
        for g in got:
            total = total + g.astype(jnp.float32).reshape(total.shape)
    return total.astype(jnp.bfloat16)


def solution(mesh):
    placed = (
        P(("groups", "fsdp", "ep"), None),
        P("fsdp", "ep"),
        P("fsdp", "ep"),
        P("ep", "fsdp"),
        P(),
        P(None, "groups", None),
        P(None, "groups", None),
    )
    return jax.shard_map(
        body,
        mesh=mesh,
        in_specs=placed,
        out_specs=P(("groups", "fsdp", "ep"), None),
        check_vma=False,
    )
```

```python
import functools

import jax
import jax.numpy as jnp
from jax import lax
from jax.experimental import pallas as pl
from jax.experimental.pallas import tpu as pltpu
from jax.sharding import PartitionSpec as P

VMEM_LIMIT = 48 * 2**20


def swap_cores(x):
    return lax.ppermute(x, "fsdp", [(0, 1), (1, 0)])


def exchange(x, distance, cross):
    count = lax.axis_size("ep")
    pairs = [(f * count + e, (f ^ cross) * count + (e ^ distance)) for f in range(2) for e in range(count)]
    return lax.ppermute(x, ("fsdp", "ep"), pairs)


def stages(count):
    if count == 8:
        return [[(4, 1)], [(1, 1), (2, 1), (3, 1)]]
    plan = [[(1, 1)]] if count > 1 else []
    base = 2
    while base < count:
        radix = 4 if base * 4 <= count else 2
        plan.append([(k * base, 1) for k in range(1, radix)])
        base *= radix
    return plan


def dot(a, b):
    return jnp.dot(a, b, preferred_element_type=jnp.float32)


def stage_kernel(*refs):
    count = len(refs) // 2
    copies = [pltpu.make_async_copy(refs[i], refs[count + i], refs[-1].at[i]) for i in range(count)]
    for copy in copies:
        copy.start()
    for copy in copies:
        copy.wait()


def stage(*arrays):
    return pl.pallas_call(
        stage_kernel,
        out_shape=[jax.ShapeDtypeStruct(a.shape, a.dtype) for a in arrays],
        in_specs=[pl.BlockSpec(memory_space=pltpu.HBM)] * len(arrays),
        out_specs=[pl.BlockSpec(memory_space=pltpu.VMEM)] * len(arrays),
        scratch_shapes=[pltpu.SemaphoreType.DMA((len(arrays),))],
        compiler_params=pltpu.CompilerParams(vmem_limit_bytes=VMEM_LIMIT),
        name="stage",
    )(*[pltpu.with_memory_space_constraint(a, pltpu.HBM) for a in arrays])


def experts_kernel(owners, pieces, *refs):
    row_refs = refs[:pieces]
    gate_ref, up_ref, down_ref, steer_ref, slots_ref, gates_ref, gate_far_ref, up_far_ref, down_far_ref = refs[pieces:pieces + 9]
    keep_ref = refs[pieces + 9]
    send_refs = refs[pieces + 10:2 * pieces + 9]
    rows_scr, out_scr = refs[2 * pieces + 9:]
    window_experts = slots_ref.shape[1]
    position = lax.axis_index("ep")
    half = lax.axis_index("fsdp")
    expert = position // (lax.axis_size("ep") // window_experts)
    count = len(owners)
    chunk = count // pieces
    width = gate_ref.shape[0]
    near = pl.multiple_of(half * width, 128)
    far = pl.multiple_of((1 - half) * width, 128)
    rows_scr[...] = jnp.concatenate([ref[...] for ref in row_refs], axis=0)
    x_near = rows_scr[:, pl.ds(near, width)]
    x_far = rows_scr[:, pl.ds(far, width)]
    gate_pre = dot(x_near, gate_ref[...]) + dot(x_far, gate_far_ref[...])
    up_pre = dot(x_near, up_ref[...]) + dot(x_far, up_far_ref[...])
    hidden = (gate_pre / (1.0 + jnp.exp(-gate_pre)) * up_pre).astype(jnp.bfloat16)
    row = lax.broadcasted_iota(jnp.int32, (count, 1), 0)
    offset = jnp.zeros((count, 1), jnp.int32)
    other = jnp.zeros((count, 1), jnp.int32)
    for j, (o, c) in enumerate(owners):
        if o:
            offset = jnp.where(row == j, o, offset)
        if c:
            other = jnp.where(row == j, 1, other)
    token = position ^ offset
    row_half = half ^ other
    token_gate = jnp.zeros((count, 1), jnp.float32)
    for h in range(2):
        slots = slots_ref[h, pl.ds(expert, 1), :]
        gates = gates_ref[h, pl.ds(expert, 1), :]
        found = jnp.sum(jnp.where(slots == token, gates, 0.0), axis=1, keepdims=True)
        token_gate = jnp.where(row_half == h, found, token_gate)
    out_scr[:, pl.ds(near, width)] = token_gate * dot(hidden, down_ref[...])
    out_scr[:, pl.ds(far, width)] = token_gate * dot(hidden, down_far_ref[...])
    own_gate = jnp.sum(jnp.where(slots_ref[half] == position, gates_ref[half], 0.0), axis=1, keepdims=True)
    steer = jnp.sum(own_gate * steer_ref[...].astype(jnp.float32), axis=0, keepdims=True)
    out_scr[0:1, :] = out_scr[0:1, :] + steer
    keep_ref[...] = out_scr[0:chunk, :]
    for k, ref in enumerate(send_refs):
        ref[...] = out_scr[(k + 1) * chunk:(k + 2) * chunk, :].astype(jnp.bfloat16)


def combine_kernel(*refs):
    keep_ref, own_ref, send_ref, scr = refs[0], *refs[-3:]
    total = keep_ref[...]
    for ref in refs[1:-3]:
        total = total + ref[...].astype(jnp.float32)
    own_ref[...] = total
    lanes = scr.shape[1]
    for p in range(scr.shape[0]):
        scr[p:p + 1, :] = total[1:2, p * lanes:(p + 1) * lanes]
    send_ref[...] = scr[...].astype(jnp.bfloat16)


def combine(keep, got):
    vmem = pl.BlockSpec(memory_space=pltpu.VMEM)
    send_shape = (8, keep.shape[1] // 8)
    return pl.pallas_call(
        combine_kernel,
        out_shape=[
            jax.ShapeDtypeStruct(keep.shape, jnp.float32),
            jax.ShapeDtypeStruct(send_shape, jnp.bfloat16),
        ],
        in_specs=[vmem] * (1 + len(got)),
        out_specs=[vmem] * 2,
        scratch_shapes=[pltpu.VMEM(send_shape, jnp.float32)],
        compiler_params=pltpu.CompilerParams(vmem_limit_bytes=VMEM_LIMIT),
        name="combine",
    )(keep, *got)


def body(tokens, gate_weight, up_weight, down_weight, steering, block_rows, block_gates):
    count = lax.axis_size("ep")
    width_all = tokens.shape[1]
    here = stage(gate_weight, up_weight, down_weight)
    own_row, *tables = stage(tokens, steering, block_rows, block_gates)
    rows = tokens
    owners = [(0, 0)]
    steps = stages(count)
    for i, hops in enumerate(steps):
        got = [exchange(rows, d, c) for d, c in hops]
        if not i:
            own_row, got[0], down_weight = lax.optimization_barrier((own_row, got[0], down_weight))
            far = [swap_cores(w) for w in (gate_weight, up_weight, down_weight)]
            own_row, got[0], far[0] = lax.optimization_barrier((own_row, got[0], far[0]))
            rows = own_row
        pieces = [rows] + got
        owners = owners + [(o ^ d, c ^ x) for d, x in hops for o, c in owners]
        if i + 1 < len(steps):
            rows = jnp.concatenate(pieces, axis=0)
    chunk = count // len(pieces)
    vmem = pl.BlockSpec(memory_space=pltpu.VMEM)
    outs = pl.pallas_call(
        functools.partial(experts_kernel, owners, len(pieces)),
        out_shape=[jax.ShapeDtypeStruct((chunk, width_all), jnp.float32)]
        + [jax.ShapeDtypeStruct((chunk, width_all), jnp.bfloat16)] * (len(pieces) - 1),
        in_specs=[vmem] * (len(pieces) + 9),
        out_specs=[vmem] * len(pieces),
        scratch_shapes=[pltpu.VMEM((count, width_all), jnp.bfloat16), pltpu.VMEM((count, width_all), jnp.float32)],
        compiler_params=pltpu.CompilerParams(vmem_limit_bytes=VMEM_LIMIT),
        name="experts",
    )(*pieces, *here, *tables, *far)
    total, sends = outs[0], list(outs[1:])
    ready = None
    for i, hops in enumerate(reversed(steps)):
        if i:
            chunk = total.shape[0] // (len(hops) + 1)
            sends = ready or [
                total[(k + 1) * chunk:(k + 2) * chunk].astype(jnp.bfloat16).reshape(8, -1) for k in range(len(hops))
            ]
            total = total[:chunk]
        got = [exchange(s, d, c) for s, (d, c) in reversed(list(zip(sends, hops)))]
        if total.shape[0] == 2 and not i:
            total, *ready = combine(total, got)
            continue
        ready = None
        for g in got:
            total = total + g.astype(jnp.float32).reshape(total.shape)
    return total.astype(jnp.bfloat16)


def solution(mesh):
    placed = (
        P(("groups", "fsdp", "ep"), None),
        P("fsdp", "ep"),
        P("fsdp", "ep"),
        P("ep", "fsdp"),
        P(),
        P(None, "groups", None),
        P(None, "groups", None),
    )
    return jax.shard_map(
        body,
        mesh=mesh,
        in_specs=placed,
        out_specs=P(("groups", "fsdp", "ep"), None),
        check_vma=False,
    )
```
